32 devices in a mesh: roll: 16 (over z, y, core), tensor: 2 (over x).
Axes of the slice: x: 2, y: 2, z: 4, core: 2. Of those that a mesh axis runs over, the one named last changes fastest.
Arguments:
- grad_out: bfloat16 [6144, 5120], P('roll', 'tensor'), may hold values from -6 to 6
- out_weight: bfloat16 [5120, 4096], P('roll', 'tensor'), may hold values from -0.078125 to 0.078125
- queries: bfloat16 [6144, 4096], P('roll', 'tensor'), may hold values from -6 to 6
- resp_key: bfloat16 [6144, 1024], P('roll', 'tensor'), may hold values from -5 to 5
- resp_value: bfloat16 [6144, 1024], P('roll', 'tensor'), may hold values from -5 to 5
- prefix_key: bfloat16 [64, 1024], P('roll', 'tensor'), may hold values from -5 to 5
- prefix_value: bfloat16 [64, 1024], P('roll', 'tensor'), may hold values from -5 to 5
- lengths: int32 [16], P('roll'), may hold values from 1 to 384
Outputs:
- grad_query: bfloat16 [6144, 4096], P('roll', 'tensor')
- grad_resp_key: bfloat16 [6144, 1024], P('roll', 'tensor')
- grad_resp_value: bfloat16 [6144, 1024], P('roll', 'tensor')
- grad_prefix_key: float32 [64, 1024], P('roll', 'tensor')
- grad_prefix_value: float32 [64, 1024], P('roll', 'tensor')
The draws below stay inside these ranges and needn't reach their ends.
All inputs are finite; a program needn't handle non-finite values.
Results may differ from the reference program's by a relative error of at most 0.0063.
Values may be sent and summed in bfloat16 or wider, within the bound.
A program may use at most 128 MiB of HBM per device.

```python
import jax
import jax.numpy as jnp
from jax import lax

D = 5120
HQ = 32
KVH = 8
HD = 128
ROWS = 384
RESPONSES = 16
TOKENS = 6144
PREFIX = 64


def draw_queries(key, part):
    normal_part = jnp.clip(jax.random.normal(jax.random.fold_in(key, 3), (TOKENS, HQ * HD), jnp.float32), -5.0, 5.0)
    return normal_part.astype(jnp.bfloat16)


def draw_prefix_key(key, part):
    normal_part = jnp.clip(jax.random.normal(jax.random.fold_in(key, 5), (PREFIX, KVH * HD), jnp.float32), -5.0, 5.0)
    return normal_part.astype(jnp.bfloat16)


def with_ends(entries, key, low, largest):
    longest = entries.shape.index(max(entries.shape))
    spots = []
    for shift in (0, 1):
        where = [jax.random.randint(jax.random.fold_in(key, axis), (), 0, length) for axis, length in enumerate(entries.shape)]
        where[longest] = (where[longest] + shift) % entries.shape[longest]
        spots.append(tuple(where))
    return entries.at[spots[0]].set(low).at[spots[1]].set(largest)


def block_scale(stream_key, extent, pieces, low, top_value):
    def one(axis_at, shards_of):
        draws = jax.random.uniform(jax.random.fold_in(jax.random.fold_in(stream_key, 6), axis_at), (shards_of,), jnp.float32, low / len(pieces), top_value / len(pieces))
        return jnp.repeat(jnp.exp(draws), extent[axis_at] // shards_of).reshape((-1,) + (1,) * (len(extent) - axis_at - 1))

    loudness = one(*pieces[0])
    for cut in pieces[1:]:
        loudness = loudness * one(*cut)
    return loudness


def noise(rng, shape, spread, reach, shards=(), kind=jnp.bfloat16):
    entries = spread * jax.random.normal(rng, shape, jnp.float32)
    if shards:
        entries = entries * block_scale(rng, shape, shards, -0.22, 0.18)
    return jnp.clip(entries, -reach, reach).astype(kind)


def setup_inputs(seed: int = 0) -> dict:
    streams_of = jax.random.split(jax.random.key(seed), 9)
    return {
        "grad_out": noise(streams_of[0], (TOKENS, D), 1.0, 6.0, ((0, 16), (1, 2))),
        "out_weight": noise(streams_of[1], (D, HQ * HD), D ** -0.5, 0.078125, ((0, 16), (1, 2))),
        "queries": draw_queries(jax.random.fold_in(streams_of[8], 71), 0),
        "resp_key": noise(streams_of[3], (TOKENS, KVH * HD), 1.0, 5.0, ((0, 16), (1, 2))),
        "resp_value": noise(streams_of[4], (TOKENS, KVH * HD), 1.0, 5.0, ((0, 16), (1, 2))),
        "prefix_key": draw_prefix_key(jax.random.fold_in(streams_of[8], 71), 0),
        "prefix_value": noise(streams_of[6], (PREFIX, KVH * HD), 1.0, 5.0, ((0, 16), (1, 2))),
        "lengths": with_ends(jax.random.randint(streams_of[7], (RESPONSES,), 1, ROWS + 1), jax.random.fold_in(streams_of[7], 1), 1, ROWS).astype(jnp.int32),
    }


def response_grads(queries, out_grad, resp_key, resp_value, prefix_key, prefix_value):
    row_count = queries.shape[0]
    prefix_rows = prefix_key.shape[0]
    group_size = HQ // KVH
    score_scale = HD ** -0.5
    highest = lax.Precision.HIGHEST
    all_keys = jnp.concatenate([prefix_key, resp_key], axis=0).astype(jnp.float32)
    all_values = jnp.concatenate([prefix_value, resp_value], axis=0).astype(jnp.float32)
    query_heads = queries.astype(jnp.float32).reshape(row_count, KVH, group_size, HD)
    grad_heads = out_grad.astype(jnp.float32).reshape(row_count, KVH, group_size, HD)
    key_heads = all_keys.reshape(-1, KVH, HD)
    value_heads = all_values.reshape(-1, KVH, HD)
    scores = jnp.einsum("ikgd,jkd->kgij", query_heads, key_heads, precision=highest) * score_scale
    query_place = jnp.arange(row_count, dtype=jnp.int32)[:, None]
    key_place = jnp.arange(key_heads.shape[0], dtype=jnp.int32)[None, :]
    allowed = (key_place < prefix_rows) | (key_place - prefix_rows <= query_place)
    scores = jnp.where(allowed, scores, -jnp.inf)
    row_max = jnp.max(scores, axis=-1, keepdims=True)
    shifted = jnp.exp(scores - row_max)
    soft_weights = shifted / jnp.sum(shifted, axis=-1, keepdims=True)
    weights_low = lax.optimization_barrier(soft_weights.astype(jnp.bfloat16)).astype(jnp.float32)
    prob_grad = jnp.einsum("ikgd,jkd->kgij", grad_heads, value_heads, precision=highest)
    row_delta = jnp.sum(soft_weights * prob_grad, axis=-1, keepdims=True)
    score_grad = soft_weights * (prob_grad - row_delta) * score_scale
    score_low = lax.optimization_barrier(score_grad.astype(jnp.bfloat16)).astype(jnp.float32)
    query_grad = jnp.einsum("kgij,jkd->ikgd", score_low, key_heads, precision=highest)
    key_grad = jnp.einsum("kgij,ikgd->jkd", score_low, query_heads, precision=highest).reshape(-1, KVH * HD)
    value_grad = jnp.einsum("kgij,ikgd->jkd", weights_low, grad_heads, precision=highest).reshape(-1, KVH * HD)
    return (query_grad.reshape(row_count, HQ * HD).astype(jnp.bfloat16),
            key_grad[prefix_rows:].astype(jnp.bfloat16),
            value_grad[prefix_rows:].astype(jnp.bfloat16),
            key_grad[:prefix_rows],
            value_grad[:prefix_rows])


def reference(grad_out, out_weight, queries, resp_key, resp_value, prefix_key, prefix_value, lengths):
    token_count = grad_out.shape[0]
    position = jnp.arange(token_count, dtype=jnp.int32)
    owner_index = position // ROWS
    valid_rows = (position % ROWS < lengths[owner_index]).astype(jnp.float32)
    projected = jnp.dot(grad_out, out_weight, preferred_element_type=jnp.float32)
    out_grad = (projected * valid_rows[:, None]).astype(jnp.bfloat16)

    def one_response(running, response):
        start_row = response * ROWS

        def rows_of(array):
            return lax.dynamic_slice_in_dim(array, start_row, ROWS, 0)

        query_grad, key_grad, value_grad, prefix_key_part, prefix_value_part = response_grads(
            rows_of(queries), rows_of(out_grad), rows_of(resp_key), rows_of(resp_value),
            prefix_key, prefix_value)
        return (running[0] + prefix_key_part, running[1] + prefix_value_part), (query_grad, key_grad, value_grad)

    initial = (jnp.zeros(prefix_key.shape, jnp.float32), jnp.zeros(prefix_value.shape, jnp.float32))
    sums, grads = lax.scan(one_response, initial, jnp.arange(lengths.shape[0], dtype=jnp.int32))
    grad_query = grads[0].reshape(token_count, HQ * HD)
    grad_resp_key = grads[1].reshape(token_count, KVH * HD)
    grad_resp_value = grads[2].reshape(token_count, KVH * HD)
    return grad_query, grad_resp_key, grad_resp_value, sums[0], sums[1]
```

```python
import functools

import jax
import jax.numpy as jnp
from jax import lax
from jax.experimental import pallas as pl
from jax.experimental.pallas import tpu as pltpu
from jax.sharding import PartitionSpec as P

HD = 128
MESH = pl.DeviceIdType.MESH
NT = (((1,), (1,)), ((), ()))
TN = (((0,), (0,)), ((), ()))


def grid_of(roll):
    cores = 2 if roll % 2 == 0 else 1
    chips = roll // cores
    ys = 1
    while 4 * ys * ys <= chips and chips % (2 * ys) == 0:
        ys *= 2
    return chips // ys, ys, cores


def kernel(
    R, T,
    len_ref, g_hbm, w_hbm, pkv_hbm, q_ref, k_ref, v_ref,
    oq_ref, ok_ref, ov_ref, opk_ref, opv_ref,
    wbuf, gbuf, pbuf, pfull, og, dk, dv, rs_src, rs_in,
    lsem, glsem, plsem, rsem, ssem, grsem, gssem, prsem, pssem, rrsem, rssem,
):
    Z, Y, C = grid_of(R)
    NR, _, WR, SUB = wbuf.shape
    NK = rs_in.shape[0]
    PR = pbuf.shape[1]
    PF = R * PR
    rows = q_ref.shape[0]
    group = q_ref.shape[1] // k_ref.shape[1]
    gw = group * HD
    per_head = gw // SUB
    kw = k_ref.shape[1]
    me = lax.axis_index("roll")
    tp = lax.axis_index("tensor")
    c = lax.rem(me, C)
    y = lax.rem(me // C, Y)
    z = me // (C * Y)
    items = Z * Y
    lag = (Z - 1) + (Y - 1)
    every = 6

    def rid(zz, yy, cc):
        return (zz * Y + yy) * C + cc

    own_w = [
        pltpu.make_async_copy(w_hbm.at[:, pl.ds(r * SUB, SUB)], wbuf.at[r, me], lsem.at[r])
        for r in range(NR)
    ]
    own_g = pltpu.make_async_copy(g_hbm, gbuf.at[tp], glsem)
    own_p = pltpu.make_async_copy(pkv_hbm, pbuf.at[me], plsem)
    for cp in own_w:
        cp.start()
    own_g.start()
    own_p.start()

    barrier = pltpu.get_barrier_semaphore()

    @pl.loop(1, R)
    def _(d):
        pl.semaphore_signal(
            barrier, inc=1, device_id={"roll": lax.rem(me + d, R)}, device_id_type=MESH)

    for t in range(1, T):
        pl.semaphore_signal(
            barrier, inc=1, device_id={"tensor": lax.rem(tp + t, T)}, device_id_type=MESH)
    pl.semaphore_wait(barrier, R - 1 + T - 1)

    def w_copy(kind, j, r, o, dst):
        return pltpu.make_async_remote_copy(
            src_ref=wbuf.at[r, o], dst_ref=wbuf.at[r, o],
            send_sem=ssem.at[kind, r, j], recv_sem=rsem.at[r, o],
            device_id={"roll": dst}, device_id_type=MESH)

    def place(j):
        return lax.rem(z + j // Y, Z), lax.rem(y + lax.rem(j, Y), Y)

    def sends(j, r, act):
        zz, yy = place(j)
        o = rid(zz, yy, c)
        crossed = lax.rem(r, every) == every // 2
        along_z = jnp.logical_or(yy == y, crossed)
        along_y = jnp.logical_or(zz == z, jnp.logical_not(crossed))

        def step(kind, cond, dst):
            @pl.when(cond)
            def _():
                act(w_copy(kind, j, r, o, dst))

        if Y > 1:
            step(0, along_y & (yy <= y) & (y + 1 < Y), rid(z, y + 1, c))
            step(1, along_y & (yy >= y) & (y > 0), rid(z, y - 1, c))
        if Z > 1:
            step(2, along_z & (zz <= z) & (z + 1 < Z), rid(z + 1, y, c))
            step(3, along_z & (zz >= z) & (z > 0), rid(z - 1, y, c))
        if C > 1:
            act(w_copy(4, j, r, o, rid(z, y, 1 - c)))

    def g_copy(t):
        return pltpu.make_async_remote_copy(
            src_ref=gbuf.at[tp], dst_ref=gbuf.at[tp], send_sem=gssem.at[t],
            recv_sem=grsem.at[tp], device_id={"tensor": lax.rem(tp + t, T)},
            device_id_type=MESH)

    def g_arrival(t):
        src = lax.rem(tp + t, T)
        return pltpu.make_async_remote_copy(
            src_ref=gbuf.at[src], dst_ref=gbuf.at[src], send_sem=gssem.at[t],
            recv_sem=grsem.at[src], device_id={"tensor": src}, device_id_type=MESH)

    def p_copy(slot, d, o):
        return pltpu.make_async_remote_copy(
            src_ref=pbuf.at[slot], dst_ref=pbuf.at[slot], send_sem=pssem.at[d],
            recv_sem=prsem.at[slot], device_id={"roll": o}, device_id_type=MESH)

    def r_copy(h, src, slot, o):
        return pltpu.make_async_remote_copy(
            src_ref=rs_src.at[h, src], dst_ref=rs_in.at[h, slot], send_sem=rssem.at[h, src],
            recv_sem=rrsem.at[h, slot], device_id={"roll": o}, device_id_type=MESH)

    def project(r):
        total = None
        for t in range(T):
            n = R // T
            part = jnp.dot(
                gbuf[t], wbuf[r, t * n:(t + 1) * n].reshape(n * WR, SUB),
                preferred_element_type=jnp.float32)
            total = part if total is None else total + part
        row = lax.broadcasted_iota(jnp.int32, (rows, SUB), 0)
        valid = (row < len_ref[0]).astype(jnp.float32)
        og[lax.rem(r, per_head)] = (total * valid).astype(jnp.bfloat16)

    def attend(h):
        scale = HD ** -0.5
        power = scale * 1.4426950408889634
        kcols = pl.ds(pl.multiple_of(h * HD, HD), HD)
        vcols = pl.ds(pl.multiple_of(kw + h * HD, HD), HD)
        kall = jnp.concatenate([pfull[:, kcols].astype(jnp.bfloat16), k_ref[:, kcols]], axis=0)
        vall = jnp.concatenate([pfull[:, vcols].astype(jnp.bfloat16), v_ref[:, kcols]], axis=0)
        br = min(128, rows)
        nb = rows // br
        key = lax.broadcasted_iota(jnp.int32, (br, group * br), 0)
        row = lax.rem(lax.broadcasted_iota(jnp.int32, (br, group * br), 1), br)
        allowed = key <= row
        for i in range(nb - 1, -1, -1):
            span = slice(i * br, (i + 1) * br)
            nk = PF + (i + 1) * br
            kc, vc = kall[:nk], vall[:nk]
            qs, gs = [], []
            for a in range(group):
                qs.append(q_ref[span, pl.ds(pl.multiple_of(h * gw + a * HD, HD), HD)])
                lane = a * HD
                gs.append(og[lane // SUB, span, lane % SUB:lane % SUB + HD])
            qi = jnp.concatenate(qs, axis=0)
            gi = jnp.concatenate(gs, axis=0)
            s = lax.dot_general(kc, qi, NT, preferred_element_type=jnp.float32)
            s = jnp.concatenate([s[:nk - br], jnp.where(allowed, s[nk - br:], -jnp.inf)], axis=0)
            top = jnp.max(s, axis=0, keepdims=True)
            e = jnp.exp2((s - top) * power)
            inv = 1.0 / jnp.sum(e, axis=0, keepdims=True)
            dp = lax.dot_general(vc, gi, NT, preferred_element_type=jnp.float32)
            w = e * inv
            delta = jnp.sum(w * dp, axis=0, keepdims=True)
            wl = w.astype(jnp.bfloat16)
            ds = (w * (dp - delta) * scale).astype(jnp.bfloat16)
            dki = jnp.dot(ds, qi, preferred_element_type=jnp.float32)
            dvi = jnp.dot(wl, gi, preferred_element_type=jnp.float32)
            if i == nb - 1:
                dk[...] = dki
                dv[...] = dvi
            else:
                dk[:nk] += dki
                dv[:nk] += dvi
            dq = lax.dot_general(kc, ds, TN, preferred_element_type=jnp.float32).T
            for a in range(group):
                oq_ref[span, pl.ds(pl.multiple_of(h * gw + a * HD, HD), HD)] = (
                    dq[a * br:(a + 1) * br].astype(jnp.bfloat16))
        for o in range(R):
            rs_src[h, o, :, :HD] = dk[o * PR:(o + 1) * PR]
            rs_src[h, o, :, HD:] = dv[o * PR:(o + 1) * PR]
        ok_ref[:, kcols] = dk[PF:].astype(jnp.bfloat16)
        ov_ref[:, kcols] = dv[PF:].astype(jnp.bfloat16)
        rs_in[h, me] = rs_src[h, me]

        @pl.loop(1, R)
        def _(d):
            o = lax.rem(me + d, R)
            r_copy(h, o, me, o).start()

    own_p.wait()
    own_g.wait()
    for cp in own_w:
        cp.wait()

    def step(s, carry):
        def one(j, carry):
            zz, yy = place(j)
            r = s - jnp.abs(zz - z) - jnp.abs(yy - y)

            @pl.when((r >= 0) & (r < NR))
            def _():
                @pl.when(j > 0)
                def _():
                    w_copy(4, j, r, rid(zz, yy, c), rid(z, y, 1 - c)).wait_recv()

                sends(j, r, lambda cp: cp.start())

            return carry

        lax.fori_loop(0, items, one, 0)

        @pl.when(s == 0)
        def _():
            for t in range(1, T):
                g_copy(t).start()

            @pl.loop(1, R)
            def _(d):
                p_copy(me, d, lax.rem(me + d, R)).start()

        ready = s - lag

        @pl.when(ready >= 0)
        def _():
            if C > 1:
                @pl.loop(0, items)
                def _(j):
                    zz, yy = place(j)
                    w_copy(4, j, ready, rid(zz, yy, 1 - c), rid(z, y, 1 - c)).wait_recv()

            @pl.when(ready == 0)
            def _():
                for t in range(1, T):
                    g_arrival(t).wait_recv()

                @pl.loop(1, R)
                def _(d):
                    o = lax.rem(me + d, R)
                    p_copy(o, d, o).wait_recv()

                for o in range(R):
                    pfull[o * PR:(o + 1) * PR, :] = pbuf[o].astype(jnp.float32)

            project(ready)

            @pl.when(lax.rem(ready, per_head) == per_head - 1)
            def _():
                attend(ready // per_head)

        return carry

    lax.fori_loop(0, NR + lag, step, 0)

    @pl.loop(0, NK)
    def _(h):
        @pl.loop(1, R)
        def _(d):
            o = lax.rem(me + d, R)
            r_copy(h, o, o, o).wait_recv()

    for h in range(NK):
        total = rs_in[h, 0]
        for o in range(1, R):
            total = total + rs_in[h, o]
        opk_ref[:, h * HD:(h + 1) * HD] = total[:, :HD]
        opv_ref[:, h * HD:(h + 1) * HD] = total[:, HD:]

    @pl.loop(0, NR)
    def _(r):
        @pl.loop(0, items)
        def _(j):
            sends(j, r, lambda cp: cp.wait_send())

    for t in range(1, T):
        g_copy(t).wait_send()

    @pl.loop(1, R)
    def _(d):
        o = lax.rem(me + d, R)
        p_copy(me, d, o).wait_send()

        @pl.loop(0, NK)
        def _(h):
            r_copy(h, o, me, o).wait_send()


def body(R, T, grad_out, out_weight, queries, resp_key, resp_value, prefix_key, prefix_value, lengths):
    rows, dcols = grad_out.shape
    wr, cols = out_weight.shape
    kw = resp_key.shape[1]
    pr = prefix_key.shape[0]
    nk = kw // HD
    gw = cols // nk
    sub = gw // 2 if gw % 256 == 0 else gw
    nr = cols // sub
    Z, Y, C = grid_of(R)
    vm = pl.BlockSpec(memory_space=pltpu.VMEM)
    hb = pl.BlockSpec(memory_space=pl.ANY)
    dma = pltpu.SemaphoreType.DMA
    pkv = jnp.concatenate([prefix_key, prefix_value], axis=1)
    bf, f32 = jnp.bfloat16, jnp.float32
    return pl.pallas_call(
        functools.partial(kernel, R, T),
        out_shape=(
            jax.ShapeDtypeStruct((rows, cols), bf),
            jax.ShapeDtypeStruct((rows, kw), bf),
            jax.ShapeDtypeStruct((rows, kw), bf),
            jax.ShapeDtypeStruct((pr, kw), f32),
            jax.ShapeDtypeStruct((pr, kw), f32),
        ),
        in_specs=[pl.BlockSpec(memory_space=pltpu.SMEM), hb, hb, hb, vm, vm, vm],
        out_specs=(vm,) * 5,
        scratch_shapes=[
            pltpu.VMEM((nr, R, wr, sub), bf),
            pltpu.VMEM((T, rows, dcols), bf),
            pltpu.VMEM((R, pr, 2 * kw), bf),
            pltpu.VMEM((R * pr, 2 * kw), f32),
            pltpu.VMEM((gw // sub, rows, sub), bf),
            pltpu.VMEM((R * pr + rows, HD), f32),
            pltpu.VMEM((R * pr + rows, HD), f32),
            pltpu.VMEM((nk, R, pr, 2 * HD), f32),
            pltpu.VMEM((nk, R, pr, 2 * HD), f32),
            dma((nr,)), dma, dma,
            dma((nr, R)), dma((5, nr, Z * Y)),
            dma((T,)), dma((T,)),
            dma((R,)), dma((R,)),
            dma((nk, R)), dma((nk, R)),
        ],
        compiler_params=pltpu.CompilerParams(
            collective_id=0, has_side_effects=True, vmem_limit_bytes=60 * 1024 * 1024),
        name="gather_project_attend",
    )(lengths, grad_out, out_weight, pkv, queries, resp_key, resp_value)


def solution(mesh):
    spec = P("roll", "tensor")
    return jax.shard_map(
        functools.partial(body, mesh.shape["roll"], mesh.shape["tensor"]),
        mesh=mesh,
        in_specs=(spec,) * 7 + (P("roll"),),
        out_specs=(spec,) * 5,
        check_vma=False,
    )
```

```python
import functools

import jax
import jax.numpy as jnp
from jax import lax
from jax.experimental import pallas as pl
from jax.experimental.pallas import tpu as pltpu
from jax.sharding import PartitionSpec as P

HD = 128
MESH = pl.DeviceIdType.MESH
NT = (((1,), (1,)), ((), ()))
TN = (((0,), (0,)), ((), ()))


def grid_of(roll):
    cores = 2 if roll % 2 == 0 else 1
    chips = roll // cores
    ys = 1
    while 4 * ys * ys <= chips and chips % (2 * ys) == 0:
        ys *= 2
    return chips // ys, ys, cores


def kernel(
    R, T,
    len_ref, g_hbm, w_hbm, pk_hbm, pv_hbm, q_ref, k_ref, v_ref,
    oq_ref, ok_ref, ov_ref, opk_ref, opv_ref,
    wbuf, gbuf, pbuf, pfull, og, dk, dv, rs_src, rs_in,
    lsem, glsem, plsem, rsem, ssem, grsem, gssem, prsem, pssem, rrsem, rssem,
):
    Z, Y, C = grid_of(R)
    NR, _, WR, SUB = wbuf.shape
    NK = rs_in.shape[0]
    PR = pbuf.shape[1]
    PF = R * PR
    rows = q_ref.shape[0]
    group = q_ref.shape[1] // k_ref.shape[1]
    gw = group * HD
    per_head = gw // SUB
    kw = k_ref.shape[1]
    me = lax.axis_index("roll")
    tp = lax.axis_index("tensor")
    c = lax.rem(me, C)
    y = lax.rem(me // C, Y)
    z = me // (C * Y)
    items = Z * Y
    lag = (Z - 1) + (Y - 1)
    every = 6

    def rid(zz, yy, cc):
        return (zz * Y + yy) * C + cc

    own_w = [
        pltpu.make_async_copy(w_hbm.at[:, pl.ds(r * SUB, SUB)], wbuf.at[r, me], lsem.at[r])
        for r in range(NR)
    ]
    own_g = pltpu.make_async_copy(g_hbm, gbuf.at[tp], glsem)
    own_p = [
        pltpu.make_async_copy(pk_hbm, pbuf.at[me, :, pl.ds(0, kw)], plsem.at[0]),
        pltpu.make_async_copy(pv_hbm, pbuf.at[me, :, pl.ds(kw, kw)], plsem.at[1]),
    ]
    for cp in own_w:
        cp.start()
    own_g.start()
    for cp in own_p:
        cp.start()

    barrier = pltpu.get_barrier_semaphore()

    @pl.loop(1, R)
    def _(d):
        pl.semaphore_signal(
            barrier, inc=1, device_id={"roll": lax.rem(me + d, R)}, device_id_type=MESH)

    for t in range(1, T):
        pl.semaphore_signal(
            barrier, inc=1, device_id={"tensor": lax.rem(tp + t, T)}, device_id_type=MESH)
    pl.semaphore_wait(barrier, R - 1 + T - 1)

    def w_copy(kind, j, r, o, dst):
        return pltpu.make_async_remote_copy(
            src_ref=wbuf.at[r, o], dst_ref=wbuf.at[r, o],
            send_sem=ssem.at[kind, r, j], recv_sem=rsem.at[r, o],
            device_id={"roll": dst}, device_id_type=MESH)

    def place(j):
        return lax.rem(z + j // Y, Z), lax.rem(y + lax.rem(j, Y), Y)

    def sends(j, r, act):
        zz, yy = place(j)
        o = rid(zz, yy, c)
        crossed = lax.rem(r, every) == every // 2
        along_z = jnp.logical_or(yy == y, crossed)
        along_y = jnp.logical_or(zz == z, jnp.logical_not(crossed))

        def step(kind, cond, dst):
            @pl.when(cond)
            def _():
                act(w_copy(kind, j, r, o, dst))

        if Y > 1:
            step(0, along_y & (yy <= y) & (y + 1 < Y), rid(z, y + 1, c))
            step(1, along_y & (yy >= y) & (y > 0), rid(z, y - 1, c))
        if Z > 1:
            step(2, along_z & (zz <= z) & (z + 1 < Z), rid(z + 1, y, c))
            step(3, along_z & (zz >= z) & (z > 0), rid(z - 1, y, c))
        if C > 1:
            act(w_copy(4, j, r, o, rid(z, y, 1 - c)))

    def g_copy(t):
        return pltpu.make_async_remote_copy(
            src_ref=gbuf.at[tp], dst_ref=gbuf.at[tp], send_sem=gssem.at[t],
            recv_sem=grsem.at[tp], device_id={"tensor": lax.rem(tp + t, T)},
            device_id_type=MESH)

    def g_arrival(t):
        src = lax.rem(tp + t, T)
        return pltpu.make_async_remote_copy(
            src_ref=gbuf.at[src], dst_ref=gbuf.at[src], send_sem=gssem.at[t],
            recv_sem=grsem.at[src], device_id={"tensor": src}, device_id_type=MESH)

    def p_copy(slot, d, o):
        return pltpu.make_async_remote_copy(
            src_ref=pbuf.at[slot], dst_ref=pbuf.at[slot], send_sem=pssem.at[d],
            recv_sem=prsem.at[slot], device_id={"roll": o}, device_id_type=MESH)

    def r_copy(h, src, slot, o):
        return pltpu.make_async_remote_copy(
            src_ref=rs_src.at[h, src], dst_ref=rs_in.at[h, slot], send_sem=rssem.at[h, src],
            recv_sem=rrsem.at[h, slot], device_id={"roll": o}, device_id_type=MESH)

    def project(r):
        total = None
        for t in range(T):
            n = R // T
            part = jnp.dot(
                gbuf[t], wbuf[r, t * n:(t + 1) * n].reshape(n * WR, SUB),
                preferred_element_type=jnp.float32)
            total = part if total is None else total + part
        row = lax.broadcasted_iota(jnp.int32, (rows, SUB), 0)
        valid = (row < len_ref[0]).astype(jnp.float32)
        og[lax.rem(r, per_head)] = (total * valid).astype(jnp.bfloat16)

    def attend(h):
        scale = HD ** -0.5
        power = scale * 1.4426950408889634
        kcols = pl.ds(pl.multiple_of(h * HD, HD), HD)
        vcols = pl.ds(pl.multiple_of(kw + h * HD, HD), HD)
        kall = jnp.concatenate([pfull[:, kcols].astype(jnp.bfloat16), k_ref[:, kcols]], axis=0)
        vall = jnp.concatenate([pfull[:, vcols].astype(jnp.bfloat16), v_ref[:, kcols]], axis=0)
        br = min(128, rows)
        nb = rows // br
        key = lax.broadcasted_iota(jnp.int32, (br, group * br), 0)
        row = lax.rem(lax.broadcasted_iota(jnp.int32, (br, group * br), 1), br)
        allowed = key <= row
        for i in range(nb - 1, -1, -1):
            span = slice(i * br, (i + 1) * br)
            nk = PF + (i + 1) * br
            kc, vc = kall[:nk], vall[:nk]
            qs, gs = [], []
            for a in range(group):
                qs.append(q_ref[span, pl.ds(pl.multiple_of(h * gw + a * HD, HD), HD)])
                lane = a * HD
                gs.append(og[lane // SUB, span, lane % SUB:lane % SUB + HD])
            qi = jnp.concatenate(qs, axis=0)
            gi = jnp.concatenate(gs, axis=0)
            s = lax.dot_general(kc, qi, NT, preferred_element_type=jnp.float32)
            s = jnp.concatenate([s[:nk - br], jnp.where(allowed, s[nk - br:], -jnp.inf)], axis=0)
            top = jnp.max(s, axis=0, keepdims=True)
            e = jnp.exp2((s - top) * power)
            inv = 1.0 / jnp.sum(e, axis=0, keepdims=True)
            dp = lax.dot_general(vc, gi, NT, preferred_element_type=jnp.float32)
            w = e * inv
            delta = jnp.sum(w * dp, axis=0, keepdims=True)
            wl = w.astype(jnp.bfloat16)
            ds = (w * (dp - delta) * scale).astype(jnp.bfloat16)
            dki = jnp.dot(ds, qi, preferred_element_type=jnp.float32)
            dvi = jnp.dot(wl, gi, preferred_element_type=jnp.float32)
            if i == nb - 1:
                dk[...] = dki
                dv[...] = dvi
            else:
                dk[:nk] += dki
                dv[:nk] += dvi
            dq = lax.dot_general(kc, ds, TN, preferred_element_type=jnp.float32).T
            for a in range(group):
                oq_ref[span, pl.ds(pl.multiple_of(h * gw + a * HD, HD), HD)] = (
                    dq[a * br:(a + 1) * br].astype(jnp.bfloat16))
        for o in range(R):
            rs_src[h, o, :, :HD] = dk[o * PR:(o + 1) * PR]
            rs_src[h, o, :, HD:] = dv[o * PR:(o + 1) * PR]
        ok_ref[:, kcols] = dk[PF:].astype(jnp.bfloat16)
        ov_ref[:, kcols] = dv[PF:].astype(jnp.bfloat16)
        rs_in[h, me] = rs_src[h, me]

        @pl.loop(1, R)
        def _(d):
            o = lax.rem(me + d, R)
            r_copy(h, o, me, o).start()

    for cp in own_p:
        cp.wait()
    own_g.wait()
    for cp in own_w:
        cp.wait()

    def step(s, carry):
        def one(j, carry):
            zz, yy = place(j)
            r = s - jnp.abs(zz - z) - jnp.abs(yy - y)

            @pl.when((r >= 0) & (r < NR))
            def _():
                @pl.when(j > 0)
                def _():
                    w_copy(4, j, r, rid(zz, yy, c), rid(z, y, 1 - c)).wait_recv()

                sends(j, r, lambda cp: cp.start())

            return carry

        lax.fori_loop(0, items, one, 0)

        @pl.when(s == 0)
        def _():
            for t in range(1, T):
                g_copy(t).start()

            @pl.loop(1, R)
            def _(d):
                p_copy(me, d, lax.rem(me + d, R)).start()

        ready = s - lag

        @pl.when(ready >= 0)
        def _():
            if C > 1:
                @pl.loop(0, items)
                def _(j):
                    zz, yy = place(j)
                    w_copy(4, j, ready, rid(zz, yy, 1 - c), rid(z, y, 1 - c)).wait_recv()

            @pl.when(ready == 0)
            def _():
                for t in range(1, T):
                    g_arrival(t).wait_recv()

                @pl.loop(1, R)
                def _(d):
                    o = lax.rem(me + d, R)
                    p_copy(o, d, o).wait_recv()

                for o in range(R):
                    pfull[o * PR:(o + 1) * PR, :] = pbuf[o].astype(jnp.float32)

            project(ready)

            @pl.when(lax.rem(ready, per_head) == per_head - 1)
            def _():
                attend(ready // per_head)

        return carry

    lax.fori_loop(0, NR + lag, step, 0)

    @pl.loop(0, NK)
    def _(h):
        @pl.loop(1, R)
        def _(d):
            o = lax.rem(me + d, R)
            r_copy(h, o, o, o).wait_recv()

    for h in range(NK):
        total = rs_in[h, 0]
        for o in range(1, R):
            total = total + rs_in[h, o]
        opk_ref[:, h * HD:(h + 1) * HD] = total[:, :HD]
        opv_ref[:, h * HD:(h + 1) * HD] = total[:, HD:]

    @pl.loop(0, NR)
    def _(r):
        @pl.loop(0, items)
        def _(j):
            sends(j, r, lambda cp: cp.wait_send())

    for t in range(1, T):
        g_copy(t).wait_send()

    @pl.loop(1, R)
    def _(d):
        o = lax.rem(me + d, R)
        p_copy(me, d, o).wait_send()

        @pl.loop(0, NK)
        def _(h):
            r_copy(h, o, me, o).wait_send()


def hand_out(*refs):
    half = len(refs) // 2
    for src, dst in zip(refs[:half], refs[half:]):
        dst[...] = src[...]


def body(R, T, grad_out, out_weight, queries, resp_key, resp_value, prefix_key, prefix_value, lengths):
    rows, dcols = grad_out.shape
    wr, cols = out_weight.shape
    kw = resp_key.shape[1]
    pr = prefix_key.shape[0]
    nk = kw // HD
    gw = cols // nk
    sub = gw // 2 if gw % 256 == 0 else gw
    nr = cols // sub
    Z, Y, C = grid_of(R)
    vm = pl.BlockSpec(memory_space=pltpu.VMEM)
    hb = pl.BlockSpec(memory_space=pl.ANY)
    dma = pltpu.SemaphoreType.DMA
    bf, f32 = jnp.bfloat16, jnp.float32
    grads = pl.pallas_call(
        functools.partial(kernel, R, T),
        out_shape=(
            jax.ShapeDtypeStruct((rows, cols), bf),
            jax.ShapeDtypeStruct((rows, kw), bf),
            jax.ShapeDtypeStruct((rows, kw), bf),
            jax.ShapeDtypeStruct((pr, kw), f32),
            jax.ShapeDtypeStruct((pr, kw), f32),
        ),
        in_specs=[pl.BlockSpec(memory_space=pltpu.SMEM), hb, hb, hb, hb, vm, vm, vm],
        out_specs=(vm,) * 5,
        scratch_shapes=[
            pltpu.VMEM((nr, R, wr, sub), bf),
            pltpu.VMEM((T, rows, dcols), bf),
            pltpu.VMEM((R, pr, 2 * kw), bf),
            pltpu.VMEM((R * pr, 2 * kw), f32),
            pltpu.VMEM((gw // sub, rows, sub), bf),
            pltpu.VMEM((R * pr + rows, HD), f32),
            pltpu.VMEM((R * pr + rows, HD), f32),
            pltpu.VMEM((nk, R, pr, 2 * HD), f32),
            pltpu.VMEM((nk, R, pr, 2 * HD), f32),
            dma((nr,)), dma, dma((2,)),
            dma((nr, R)), dma((5, nr, Z * Y)),
            dma((T,)), dma((T,)),
            dma((R,)), dma((R,)),
            dma((nk, R)), dma((nk, R)),
        ],
        compiler_params=pltpu.CompilerParams(
            collective_id=0, has_side_effects=True, vmem_limit_bytes=60 * 1024 * 1024),
        name="gather_project_attend",
    )(lengths, grad_out, out_weight, prefix_key, prefix_value, queries, resp_key, resp_value)
    steps = 3 if rows % 48 == 0 else 1
    specs = [
        pl.BlockSpec((rows // steps, g.shape[1]), lambda i: (i, 0)) if g.shape[0] == rows
        else pl.BlockSpec(g.shape, lambda i: (0, 0))
        for g in grads
    ]
    return pl.pallas_call(
        hand_out,
        out_shape=tuple(jax.ShapeDtypeStruct(g.shape, g.dtype) for g in grads),
        grid=(steps,),
        in_specs=specs,
        out_specs=tuple(specs),
        name="hand_out",
    )(*grads)


def solution(mesh):
    spec = P("roll", "tensor")
    return jax.shard_map(
        functools.partial(body, mesh.shape["roll"], mesh.shape["tensor"]),
        mesh=mesh,
        in_specs=(spec,) * 7 + (P("roll"),),
        out_specs=(spec,) * 5,
        check_vma=False,
    )
```

```python
import functools

import jax
import jax.numpy as jnp
from jax import lax
from jax.experimental import pallas as pl
from jax.experimental.pallas import tpu as pltpu
from jax.sharding import PartitionSpec as P

HD = 128
MESH = pl.DeviceIdType.MESH
NT = (((1,), (1,)), ((), ()))
TN = (((0,), (0,)), ((), ()))


def grid_of(roll):
    cores = 2 if roll % 2 == 0 else 1
    chips = roll // cores
    ys = 1
    while 4 * ys * ys <= chips and chips % (2 * ys) == 0:
        ys *= 2
    return chips // ys, ys, cores


def kernel(
    R, T,
    len_ref, g_hbm, w_hbm, pk_hbm, pv_hbm, q_hbm, k_hbm, v_hbm,
    oq_ref, ok_ref, ov_ref, opk_ref, opv_ref,
    q_ref, k_ref, v_ref, qkvsem, wbuf, gbuf, pbuf, pfull, og, dk, dv, rs_src, rs_in,
    lsem, glsem, plsem, rsem, ssem, grsem, gssem, prsem, pssem, rrsem, rssem,
):
    Z, Y, C = grid_of(R)
    NR, _, WR, SUB = wbuf.shape
    NK = rs_in.shape[0]
    PR = pbuf.shape[1]
    PF = R * PR
    rows = q_ref.shape[0]
    group = q_ref.shape[1] // k_ref.shape[1]
    gw = group * HD
    per_head = gw // SUB
    kw = k_ref.shape[1]
    me = lax.axis_index("roll")
    tp = lax.axis_index("tensor")
    c = lax.rem(me, C)
    y = lax.rem(me // C, Y)
    z = me // (C * Y)
    items = Z * Y
    lag = (Z - 1) + (Y - 1)
    every = 6

    def rid(zz, yy, cc):
        return (zz * Y + yy) * C + cc

    own_w = [
        pltpu.make_async_copy(w_hbm.at[:, pl.ds(r * SUB, SUB)], wbuf.at[r, me], lsem.at[r])
        for r in range(NR)
    ]
    own_g = pltpu.make_async_copy(g_hbm, gbuf.at[tp], glsem)
    own_p = [
        pltpu.make_async_copy(pk_hbm, pbuf.at[me, :, pl.ds(0, kw)], plsem.at[0]),
        pltpu.make_async_copy(pv_hbm, pbuf.at[me, :, pl.ds(kw, kw)], plsem.at[1]),
    ]
    for cp in own_w:
        cp.start()
    own_g.start()
    own_qkv = [
        pltpu.make_async_copy(src, dst, qkvsem.at[i])
        for i, (src, dst) in enumerate(((q_hbm, q_ref), (k_hbm, k_ref), (v_hbm, v_ref)))
    ]
    for cp in own_qkv:
        cp.start()
    for cp in own_p:
        cp.start()

    barrier = pltpu.get_barrier_semaphore()

    @pl.loop(1, R)
    def _(d):
        pl.semaphore_signal(
            barrier, inc=1, device_id={"roll": lax.rem(me + d, R)}, device_id_type=MESH)

    for t in range(1, T):
        pl.semaphore_signal(
            barrier, inc=1, device_id={"tensor": lax.rem(tp + t, T)}, device_id_type=MESH)
    pl.semaphore_wait(barrier, R - 1 + T - 1)

    def w_copy(kind, j, r, o, dst):
        return pltpu.make_async_remote_copy(
            src_ref=wbuf.at[r, o], dst_ref=wbuf.at[r, o],
            send_sem=ssem.at[kind, r, j], recv_sem=rsem.at[r, o],
            device_id={"roll": dst}, device_id_type=MESH)

    def place(j):
        return lax.rem(z + j // Y, Z), lax.rem(y + lax.rem(j, Y), Y)

    def sends(j, r, act):
        zz, yy = place(j)
        o = rid(zz, yy, c)
        crossed = lax.rem(r, every) == every // 2
        along_z = jnp.logical_or(yy == y, crossed)
        along_y = jnp.logical_or(zz == z, jnp.logical_not(crossed))

        def step(kind, cond, dst):
            @pl.when(cond)
            def _():
                act(w_copy(kind, j, r, o, dst))

        if Y > 1:
            step(0, along_y & (yy <= y) & (y + 1 < Y), rid(z, y + 1, c))
            step(1, along_y & (yy >= y) & (y > 0), rid(z, y - 1, c))
        if Z > 1:
            step(2, along_z & (zz <= z) & (z + 1 < Z), rid(z + 1, y, c))
            step(3, along_z & (zz >= z) & (z > 0), rid(z - 1, y, c))
        if C > 1:
            act(w_copy(4, j, r, o, rid(z, y, 1 - c)))

    def g_copy(t):
        return pltpu.make_async_remote_copy(
            src_ref=gbuf.at[tp], dst_ref=gbuf.at[tp], send_sem=gssem.at[t],
            recv_sem=grsem.at[tp], device_id={"tensor": lax.rem(tp + t, T)},
            device_id_type=MESH)

    def g_arrival(t):
        src = lax.rem(tp + t, T)
        return pltpu.make_async_remote_copy(
            src_ref=gbuf.at[src], dst_ref=gbuf.at[src], send_sem=gssem.at[t],
            recv_sem=grsem.at[src], device_id={"tensor": src}, device_id_type=MESH)

    def p_copy(slot, d, o):
        return pltpu.make_async_remote_copy(
            src_ref=pbuf.at[slot], dst_ref=pbuf.at[slot], send_sem=pssem.at[d],
            recv_sem=prsem.at[slot], device_id={"roll": o}, device_id_type=MESH)

    def r_copy(h, src, slot, o):
        return pltpu.make_async_remote_copy(
            src_ref=rs_src.at[h, src], dst_ref=rs_in.at[h, slot], send_sem=rssem.at[h, src],
            recv_sem=rrsem.at[h, slot], device_id={"roll": o}, device_id_type=MESH)

    def project(r):
        total = None
        for t in range(T):
            n = R // T
            part = jnp.dot(
                gbuf[t], wbuf[r, t * n:(t + 1) * n].reshape(n * WR, SUB),
                preferred_element_type=jnp.float32)
            total = part if total is None else total + part
        row = lax.broadcasted_iota(jnp.int32, (rows, SUB), 0)
        valid = (row < len_ref[0]).astype(jnp.float32)
        og[lax.rem(r, per_head)] = (total * valid).astype(jnp.bfloat16)

    def attend(h):
        scale = HD ** -0.5
        power = scale * 1.4426950408889634
        kcols = pl.ds(pl.multiple_of(h * HD, HD), HD)
        vcols = pl.ds(pl.multiple_of(kw + h * HD, HD), HD)
        kall = jnp.concatenate([pfull[:, kcols].astype(jnp.bfloat16), k_ref[:, kcols]], axis=0)
        vall = jnp.concatenate([pfull[:, vcols].astype(jnp.bfloat16), v_ref[:, kcols]], axis=0)
        br = min(128, rows)
        nb = rows // br
        key = lax.broadcasted_iota(jnp.int32, (br, group * br), 0)
        row = lax.rem(lax.broadcasted_iota(jnp.int32, (br, group * br), 1), br)
        allowed = key <= row
        for i in range(nb - 1, -1, -1):
            span = slice(i * br, (i + 1) * br)
            nk = PF + (i + 1) * br
            kc, vc = kall[:nk], vall[:nk]
            qs, gs = [], []
            for a in range(group):
                qs.append(q_ref[span, pl.ds(pl.multiple_of(h * gw + a * HD, HD), HD)])
                lane = a * HD
                gs.append(og[lane // SUB, span, lane % SUB:lane % SUB + HD])
            qi = jnp.concatenate(qs, axis=0)
            gi = jnp.concatenate(gs, axis=0)
            s = lax.dot_general(kc, qi, NT, preferred_element_type=jnp.float32)
            s = jnp.concatenate([s[:nk - br], jnp.where(allowed, s[nk - br:], -jnp.inf)], axis=0)
            top = jnp.max(s, axis=0, keepdims=True)
            e = jnp.exp2((s - top) * power)
            inv = 1.0 / jnp.sum(e, axis=0, keepdims=True)
            dp = lax.dot_general(vc, gi, NT, preferred_element_type=jnp.float32)
            w = e * inv
            delta = jnp.sum(w * dp, axis=0, keepdims=True)
            wl = w.astype(jnp.bfloat16)
            ds = (w * (dp - delta) * scale).astype(jnp.bfloat16)
            dki = jnp.dot(ds, qi, preferred_element_type=jnp.float32)
            dvi = jnp.dot(wl, gi, preferred_element_type=jnp.float32)
            if i == nb - 1:
                dk[...] = dki
                dv[...] = dvi
            else:
                dk[:nk] += dki
                dv[:nk] += dvi
            dq = lax.dot_general(kc, ds, TN, preferred_element_type=jnp.float32).T
            for a in range(group):
                oq_ref[span, pl.ds(pl.multiple_of(h * gw + a * HD, HD), HD)] = (
                    dq[a * br:(a + 1) * br].astype(jnp.bfloat16))
        for o in range(R):
            rs_src[h, o, :, :HD] = dk[o * PR:(o + 1) * PR]
            rs_src[h, o, :, HD:] = dv[o * PR:(o + 1) * PR]
        ok_ref[:, kcols] = dk[PF:].astype(jnp.bfloat16)
        ov_ref[:, kcols] = dv[PF:].astype(jnp.bfloat16)
        rs_in[h, me] = rs_src[h, me]

        @pl.loop(1, R)
        def _(d):
            o = lax.rem(me + d, R)
            r_copy(h, o, me, o).start()

    for cp in own_p:
        cp.wait()
    own_g.wait()
    for cp in own_qkv:
        cp.wait()
    for cp in own_w:
        cp.wait()

    def step(s, carry):
        def one(j, carry):
            zz, yy = place(j)
            r = s - jnp.abs(zz - z) - jnp.abs(yy - y)

            @pl.when((r >= 0) & (r < NR))
            def _():
                @pl.when(j > 0)
                def _():
                    w_copy(4, j, r, rid(zz, yy, c), rid(z, y, 1 - c)).wait_recv()

                sends(j, r, lambda cp: cp.start())

            return carry

        lax.fori_loop(0, items, one, 0)

        @pl.when(s == 0)
        def _():
            for t in range(1, T):
                g_copy(t).start()

            @pl.loop(1, R)
            def _(d):
                p_copy(me, d, lax.rem(me + d, R)).start()

        ready = s - lag

        @pl.when(ready >= 0)
        def _():
            if C > 1:
                @pl.loop(0, items)
                def _(j):
                    zz, yy = place(j)
                    w_copy(4, j, ready, rid(zz, yy, 1 - c), rid(z, y, 1 - c)).wait_recv()

            @pl.when(ready == 0)
            def _():
                for t in range(1, T):
                    g_arrival(t).wait_recv()

                @pl.loop(1, R)
                def _(d):
                    o = lax.rem(me + d, R)
                    p_copy(o, d, o).wait_recv()

                for o in range(R):
                    pfull[o * PR:(o + 1) * PR, :] = pbuf[o].astype(jnp.float32)

            project(ready)

            @pl.when(lax.rem(ready, per_head) == per_head - 1)
            def _():
                attend(ready // per_head)

        return carry

    lax.fori_loop(0, NR + lag, step, 0)

    @pl.loop(0, NK)
    def _(h):
        @pl.loop(1, R)
        def _(d):
            o = lax.rem(me + d, R)
            r_copy(h, o, o, o).wait_recv()

    for h in range(NK):
        total = rs_in[h, 0]
        for o in range(1, R):
            total = total + rs_in[h, o]
        opk_ref[:, h * HD:(h + 1) * HD] = total[:, :HD]
        opv_ref[:, h * HD:(h + 1) * HD] = total[:, HD:]

    @pl.loop(0, NR)
    def _(r):
        @pl.loop(0, items)
        def _(j):
            sends(j, r, lambda cp: cp.wait_send())

    for t in range(1, T):
        g_copy(t).wait_send()

    @pl.loop(1, R)
    def _(d):
        o = lax.rem(me + d, R)
        p_copy(me, d, o).wait_send()

        @pl.loop(0, NK)
        def _(h):
            r_copy(h, o, me, o).wait_send()


def hand_out(*refs):
    half = len(refs) // 2
    for src, dst in zip(refs[:half], refs[half:]):
        dst[...] = src[...]


def body(R, T, grad_out, out_weight, queries, resp_key, resp_value, prefix_key, prefix_value, lengths):
    rows, dcols = grad_out.shape
    wr, cols = out_weight.shape
    kw = resp_key.shape[1]
    pr = prefix_key.shape[0]
    nk = kw // HD
    gw = cols // nk
    sub = gw // 2 if gw % 256 == 0 else gw
    nr = cols // sub
    Z, Y, C = grid_of(R)
    vm = pl.BlockSpec(memory_space=pltpu.VMEM)
    hb = pl.BlockSpec(memory_space=pl.ANY)
    dma = pltpu.SemaphoreType.DMA
    bf, f32 = jnp.bfloat16, jnp.float32
    grads = pl.pallas_call(
        functools.partial(kernel, R, T),
        out_shape=(
            jax.ShapeDtypeStruct((rows, cols), bf),
            jax.ShapeDtypeStruct((rows, kw), bf),
            jax.ShapeDtypeStruct((rows, kw), bf),
            jax.ShapeDtypeStruct((pr, kw), f32),
            jax.ShapeDtypeStruct((pr, kw), f32),
        ),
        in_specs=[pl.BlockSpec(memory_space=pltpu.SMEM), hb, hb, hb, hb, hb, hb, hb],
        out_specs=(vm,) * 5,
        scratch_shapes=[
            pltpu.VMEM((rows, cols), bf), pltpu.VMEM((rows, kw), bf), pltpu.VMEM((rows, kw), bf), dma((3,)),
            pltpu.VMEM((nr, R, wr, sub), bf),
            pltpu.VMEM((T, rows, dcols), bf),
            pltpu.VMEM((R, pr, 2 * kw), bf),
            pltpu.VMEM((R * pr, 2 * kw), f32),
            pltpu.VMEM((gw // sub, rows, sub), bf),
            pltpu.VMEM((R * pr + rows, HD), f32),
            pltpu.VMEM((R * pr + rows, HD), f32),
            pltpu.VMEM((nk, R, pr, 2 * HD), f32),
            pltpu.VMEM((nk, R, pr, 2 * HD), f32),
            dma((nr,)), dma, dma((2,)),
            dma((nr, R)), dma((5, nr, Z * Y)),
            dma((T,)), dma((T,)),
            dma((R,)), dma((R,)),
            dma((nk, R)), dma((nk, R)),
        ],
        compiler_params=pltpu.CompilerParams(
            collective_id=0, has_side_effects=True, vmem_limit_bytes=60 * 1024 * 1024),
        name="gather_project_attend",
    )(lengths, grad_out, out_weight, prefix_key, prefix_value, queries, resp_key, resp_value)
    steps = 3 if rows % 48 == 0 else 1
    specs = [
        pl.BlockSpec((rows // steps, g.shape[1]), lambda i: (i, 0)) if g.shape[0] == rows
        else pl.BlockSpec(g.shape, lambda i: (0, 0))
        for g in grads
    ]
    return pl.pallas_call(
        hand_out,
        out_shape=tuple(jax.ShapeDtypeStruct(g.shape, g.dtype) for g in grads),
        grid=(steps,),
        in_specs=specs,
        out_specs=tuple(specs),
        name="hand_out",
    )(*grads)


def solution(mesh):
    spec = P("roll", "tensor")
    return jax.shard_map(
        functools.partial(body, mesh.shape["roll"], mesh.shape["tensor"]),
        mesh=mesh,
        in_specs=(spec,) * 7 + (P("roll"),),
        out_specs=(spec,) * 5,
        check_vma=False,
    )
```
